32 devices in a mesh: space: 8 (over z, y), members: 4 (over x, core).
Axes of the slice: x: 2, y: 2, z: 4, core: 2. Of those that a mesh axis runs over, the one named last changes fastest.
Arguments:
- latent: bfloat16 [4, 69, 15360], P('members', None, 'space'), may hold values from -40 to 40
- verifying_truth: bfloat16 [69, 15360], P(None, 'space'), may hold values from -6 to 6
- mix_weight: bfloat16 [2, 69, 69], replicated, may hold values from -0.75 to 0.75
- coefficients: float32 [2, 5, 15360], P(None, None, 'space'), may hold values from -3 to 3
- land_mask: int32 [15360], P('space'), may hold values 0 or 1
Outputs:
- latent_grad: float32 [4, 69, 15360], P('members', None, 'space')
- coefficient_grad: float32 [2, 5, 15360], P(None, None, 'space')
The draws below stay inside these ranges and needn't reach their ends.
All inputs are finite; a program needn't handle non-finite values. No bound on the sum of `land_mask` on one device may be relied on, other than what follows from the above.
Results may differ from the reference program's by a relative error of at most 0.0072.
Values may be sent and summed in bfloat16 or wider, within the bound.
A program may use at most 64 MiB of HBM per device.

```python
import math
import jax
import jax.numpy as jnp
from jax import lax

QUANTITY_NUMBER = 69
LAT = 64
LON_DEV = 30
LAYERS = 2
ENSEMBLE_SIZE = 4
CELLS = 15360
N_SPACE = 8


def draw_latent(key, part):
    region_sites = LON_DEV * LAT
    tile_count = CELLS // region_sites
    var_scale = jnp.exp(jax.random.uniform(jax.random.fold_in(key, 11), (1, QUANTITY_NUMBER, 1), jnp.float32, math.log(0.5), math.log(2.0)))
    cell_scale = jnp.exp(jax.random.uniform(jax.random.fold_in(key, 12), (1, 1, CELLS), jnp.float32, math.log(0.7), math.log(1.4)))
    member_scale = jnp.exp(jax.random.uniform(jax.random.fold_in(key, 15), (ENSEMBLE_SIZE, 1, tile_count), jnp.float32, math.log(0.3), math.log(2.0)))
    member_scale = jnp.repeat(member_scale, region_sites, axis=2)
    spacing = jax.random.uniform(jax.random.fold_in(key, 16), (1, 1, tile_count), jnp.float32, 1.0, 2.5)
    spacing = jnp.repeat(spacing, region_sites, axis=2)
    cluster_id = jax.random.randint(jax.random.fold_in(key, 17), (ENSEMBLE_SIZE, 1, tile_count), 0, 3)
    cluster_id = jnp.repeat(cluster_id, region_sites, axis=2)
    centers = jnp.clip(jax.random.normal(jax.random.fold_in(key, 18), (3, QUANTITY_NUMBER, CELLS), jnp.float32), -4.0, 4.0)
    noise = jnp.clip(jax.random.normal(jax.random.fold_in(key, 13), (ENSEMBLE_SIZE, QUANTITY_NUMBER, CELLS), jnp.float32), -4.0, 4.0)
    placed = jnp.where(cluster_id == 0, centers[0][None], jnp.where(cluster_id == 1, centers[1][None], centers[2][None]))
    base = spacing * placed + member_scale * noise
    return jnp.clip(base * var_scale * cell_scale, -40.0, 40.0).astype(jnp.bfloat16)


def place_ends(entries, own_key, smallest, top_value):
    shape = entries.shape
    place = [jax.random.randint(jax.random.fold_in(own_key, axis), (), 0, shape[axis]) for axis in range(len(shape))]
    entries = entries.at[tuple(place)].set(smallest)
    longest = shape.index(max(shape))
    place[longest] = (place[longest] + 1) % shape[longest]
    return entries.at[tuple(place)].set(top_value)


def level_of(rng, shape, pieces, smallest, high):
    loudness, own = 1.0, jax.random.fold_in(rng, 6)
    for axis_at, parts in pieces:
        steps = jnp.exp(jax.random.uniform(jax.random.fold_in(own, axis_at), (parts,), jnp.float32, smallest / len(pieces), high / len(pieces)))
        loudness = loudness * jnp.repeat(steps, shape[axis_at] // parts).reshape([-1 if axis == axis_at else 1 for axis in range(len(shape))])
    return loudness


def centred(rng, extent, width, bound, cuts=(), held_as=jnp.bfloat16):
    array = width * jax.random.normal(rng, extent, jnp.float32)
    if cuts:
        array = array * level_of(rng, extent, cuts, -0.22, 0.18)
    return jnp.clip(array, -bound, bound).astype(held_as)


def setup_inputs(seed: int = 0) -> dict:
    streams_of = jax.random.split(jax.random.key(seed), 6)
    return {
        "latent": draw_latent(jax.random.fold_in(streams_of[5], 71), 0),
        "verifying_truth": centred(streams_of[1], (QUANTITY_NUMBER, CELLS), 1.0, 6.0, ((1, 8),)),
        "mix_weight": centred(streams_of[2], (LAYERS, QUANTITY_NUMBER, QUANTITY_NUMBER), QUANTITY_NUMBER ** -0.5, 0.75),
        "coefficients": centred(streams_of[3], (LAYERS, 5, CELLS), 0.5, 3.0, ((2, 8),), jnp.float32),
        "land_mask": place_ends((jax.random.randint(streams_of[4], (CELLS,), 0, 10) < 3).astype(jnp.int32), jax.random.fold_in(streams_of[4], 1), 0, 1),
    }


gaussian_radius = 4.0


def decode_layer(member, matrix, coefficient, upper_mask, lower_mask):
    mixed_field = jnp.dot(matrix, member, preferred_element_type=jnp.float32).astype(jnp.bfloat16)
    neighbours = (mixed_field,
                  jnp.roll(mixed_field, -LAT, axis=1),
                  jnp.roll(mixed_field, LAT, axis=1),
                  jnp.roll(mixed_field, -1, axis=1) * upper_mask,
                  jnp.roll(mixed_field, 1, axis=1) * lower_mask)
    pre_activation = coefficient[0] * neighbours[0]
    for position in range(1, 5):
        pre_activation = pre_activation + coefficient[position] * neighbours[position]
    output = (member.astype(jnp.float32) + jnp.tanh(pre_activation)).astype(jnp.bfloat16)
    return output, neighbours, pre_activation


def backward_layer(cotangent, matrix, coefficient, neighbours, pre_activation, upper_mask, lower_mask):
    squashed = jnp.tanh(pre_activation)
    g_pre = cotangent * (1.0 - squashed * squashed)
    coef_terms = jnp.stack([jnp.sum(g_pre * neighbours[position].astype(jnp.float32), axis=0) for position in range(5)])
    weighted = [coefficient[position] * g_pre for position in range(5)]
    g_sum = weighted[0] + jnp.roll(weighted[1], LAT, axis=1) + jnp.roll(weighted[2], -LAT, axis=1)
    g_sum = g_sum + jnp.roll(weighted[3], 1, axis=1) * lower_mask + jnp.roll(weighted[4], -1, axis=1) * upper_mask
    g_mixed = g_sum.astype(jnp.bfloat16)
    g_in = cotangent + jnp.dot(matrix.T, g_mixed, preferred_element_type=jnp.float32)
    return g_in, coef_terms


def reference(latent, verifying_truth, mix_weight, coefficients, land_mask):
    lat_index = jnp.arange(CELLS, dtype=jnp.int32) % LAT
    upper_mask = (lat_index < LAT - 1).astype(jnp.float32)
    lower_mask = (lat_index >= 1).astype(jnp.float32)

    def decoder_apply(member):
        first = decode_layer(member, mix_weight[0], coefficients[0], upper_mask, lower_mask)[0]
        return decode_layer(first, mix_weight[1], coefficients[1], upper_mask, lower_mask)[0]

    modelled_output = lax.map(decoder_apply, latent)
    region_sites = LON_DEV * LAT
    hidden_condition = modelled_output.astype(jnp.float32).reshape(ENSEMBLE_SIZE, QUANTITY_NUMBER, N_SPACE, region_sites)
    grid_area_factor = (0.5 + land_mask.astype(jnp.float32)).reshape(N_SPACE, region_sites)
    inner_products = jnp.einsum("mctp,nctp->tmn", hidden_condition * grid_area_factor, hidden_condition, precision=lax.Precision.HIGHEST)
    local_norms = jnp.diagonal(inner_products, axis1=1, axis2=2)
    distance = (local_norms[:, :, None] + local_norms[:, None, :] - 2.0 * inner_products) / (QUANTITY_NUMBER * region_sites)
    kernel = jnp.exp(-distance / (2.0 * gaussian_radius))
    kernel_matrix_rows = jnp.sum(kernel, axis=2)
    blended = jnp.einsum("tmn,nctp->mctp", kernel, hidden_condition, precision=lax.Precision.HIGHEST)
    dispersion_part = -(jnp.transpose(kernel_matrix_rows)[:, None, :, None] * hidden_condition - blended) / ENSEMBLE_SIZE
    prediction_misfit = hidden_condition - verifying_truth.astype(jnp.float32).reshape(QUANTITY_NUMBER, N_SPACE, region_sites)[None]
    misfit = jnp.einsum("aqfd,fd->af", prediction_misfit * prediction_misfit, grid_area_factor, precision=lax.Precision.HIGHEST) / (QUANTITY_NUMBER * region_sites)
    reverse_sensitivity = jnp.exp(-misfit / (2.0 * gaussian_radius))[:, None, :, None] * prediction_misfit + dispersion_part
    reverse_sensitivity = reverse_sensitivity.reshape(ENSEMBLE_SIZE, QUANTITY_NUMBER, CELLS)

    def step(totals, inputs):
        member, cotangent = inputs
        first, neigh_first, pre_first = decode_layer(member, mix_weight[0], coefficients[0], upper_mask, lower_mask)
        second, neighbour_second, second_preactivation = decode_layer(first, mix_weight[1], coefficients[1], upper_mask, lower_mask)
        g_middle, terms_second = backward_layer(cotangent, mix_weight[1], coefficients[1], neighbour_second, second_preactivation, upper_mask, lower_mask)
        g_input, terms_first = backward_layer(g_middle, mix_weight[0], coefficients[0], neigh_first, pre_first, upper_mask, lower_mask)
        return totals + jnp.stack([terms_first, terms_second]), g_input

    totals, latent_grad = lax.scan(step, jnp.zeros((LAYERS, 5, CELLS), jnp.float32), (latent, reverse_sensitivity))
    return latent_grad, totals / ENSEMBLE_SIZE
```

```python
import functools

import jax
import jax.numpy as jnp
from jax import lax
from jax.experimental import pallas as pl
from jax.experimental.pallas import tpu as pltpu
from jax.sharding import PartitionSpec as P

LAT = 64
L = 128
gaussian_radius = 4.0
MESH = pl.DeviceIdType.MESH
f32 = jnp.float32
bf16 = jnp.bfloat16


def chunk_plan(T):
    lo, hi = 3, T - 1
    parts = []
    n = hi - lo
    if n > 0:
        pieces = 3
        edges = [lo + n * i // pieces for i in range(pieces + 1)]
        parts = [(a, b) for a, b in zip(edges[:-1], edges[1:]) if b > a]
    parts += [(1, 3), (T - 1, T + 1)]
    return parts


def kernel(
    S, M, T,
    lat_hbm, truth_hbm, w_ref, c_ref, mask_ref,
    out_ref, cg_ref,
    u0, m0, d0, u1, m1, d1, fall, truth, ch,
    gp1, g1, gm1, gp0, gm0, pk_out, pk_in, ctb,
    ls, hs, hr, ps, pr, fsx, fsp, fsr, fr, cs, cr,
):
    V = u0.shape[0]
    N = T * L
    C = M // 2
    chunks = chunk_plan(T)
    sp = lax.axis_index("space")
    me = lax.axis_index("members")
    right, left = lax.rem(sp + 1, S), lax.rem(sp + S - 1, S)
    core = lax.rem(me, 2)
    chip = me // 2
    partner = chip * 2 + (1 - core)

    def dev(s, m):
        return {"space": s, "members": m}

    def tl(k):
        return pl.ds(k * L, L)

    def rc(src, dst, a, b, d):
        return pltpu.make_async_remote_copy(
            src_ref=src, dst_ref=dst, send_sem=a, recv_sem=b,
            device_id=d, device_id_type=MESH)

    own = pltpu.make_async_copy(lat_hbm.at[0], u0.at[:, pl.ds(L, N)], ls.at[0])
    own.start()
    tru = pltpu.make_async_copy(truth_hbm, truth, ls.at[1])
    tru.start()

    barrier = pltpu.get_barrier_semaphore()
    for s in (left, right):
        pl.semaphore_signal(barrier, inc=1, device_id=dev(s, me), device_id_type=MESH)
    for j in range(1, M):
        pl.semaphore_signal(barrier, inc=1, device_id=dev(sp, lax.rem(me + j, M)), device_id_type=MESH)
    pl.semaphore_wait(barrier, M + 1)

    halo = [
        rc(lat_hbm.at[0, :, pl.ds(N - L, L)], u0.at[:, pl.ds(0, L)], hs.at[0], hr.at[0], dev(right, me)),
        rc(lat_hbm.at[0, :, pl.ds(0, L)], u0.at[:, pl.ds(N + L, L)], hs.at[1], hr.at[1], dev(left, me)),
        rc(c_ref.at[0, :, pl.ds(N - L, L)], ch.at[0], hs.at[2], hr.at[2], dev(right, me)),
        rc(c_ref.at[0, :, pl.ds(0, L)], ch.at[1], hs.at[3], hr.at[3], dev(left, me)),
    ]
    for h in halo:
        h.start()

    lane = lax.broadcasted_iota(jnp.int32, (1, L), 1)
    lat_i = lax.rem(lane, LAT)
    um = (lat_i < LAT - 1).astype(f32)
    lm = (lat_i >= 1).astype(f32)
    hi_lane = lax.broadcasted_iota(jnp.int32, (V, L), 1) >= LAT

    def coef(l, k):
        if k == 0:
            c = [ch[0, j : j + 1, :] for j in range(5)]
        elif k == T + 1:
            c = [ch[1, j : j + 1, :] for j in range(5)]
        else:
            c = [c_ref[l, j : j + 1, tl(k - 1)] for j in range(5)]
        c[3] = c[3] * um
        c[4] = c[4] * lm
        return c

    def roll64(x):
        return pltpu.roll(x, LAT, 1)

    def nbrs(m, k):
        mk = m[:, tl(k)]
        mp = m[:, tl(max(k - 1, 0))]
        mn = m[:, tl(min(k + 1, T + 1))]
        return (mk, roll64(jnp.where(hi_lane, mk, mn)), roll64(jnp.where(hi_lane, mp, mk)),
                pltpu.roll(mk, L - 1, 1), pltpu.roll(mk, 1, 1))

    w0 = w_ref[0]
    w1 = w_ref[1]

    def mix(w, src, dst, k0, k1):
        for k in range(k0, k1, 2):
            sl = pl.ds(k * L, (min(k + 2, k1) - k) * L)
            dst[:, sl] = jnp.dot(w, src[:, sl], preferred_element_type=f32).astype(bf16).astype(f32)

    def stencil(l, u, m, d, k, put):
        nb = nbrs(m, k)
        c = coef(l, k)
        pre = c[0] * nb[0]
        for j in range(1, 5):
            pre = pre + c[j] * nb[j]
        s = jnp.tanh(pre)
        put(k, (u[:, tl(k)].astype(f32) + s).astype(bf16))
        d[:, tl(k)] = 1.0 - s * s

    def put_u1(k, v):
        u1[:, tl(k)] = v

    def put_f(k, v):
        fall[me, :, tl(k - 1)] = v

    def csl(c):
        a, b = chunks[c]
        return pl.ds((a - 1) * L, (b - a) * L)

    sends = []

    def send_chunk(c):
        for j in range(1, C):
            to = lax.rem(chip + j, C) * 2 + core
            x = rc(fall.at[me, :, csl(c)], fall.at[me, :, csl(c)], fsx.at[j, c], fr.at[me, c], dev(sp, to))
            x.start()
            sends.append(x)
        x = rc(fall.at[me, :, csl(c)], fall.at[me, :, csl(c)], fsp.at[c], fr.at[me, c], dev(sp, partner))
        x.start()
        sends.append(x)

    def wait_chunk(src, c):
        rc(fall.at[src, :, csl(c)], fall.at[src, :, csl(c)], fsp.at[c], fr.at[src, c], dev(sp, partner)).wait_recv()

    own.wait()
    mix(w0, u0, m0, 1, T + 1)
    for k in range(2, T):
        stencil(0, u0, m0, d0, k, put_u1)
    mix(w1, u1, m1, 2, T)
    for c in range(len(chunks) - 2):
        for k in range(*chunks[c]):
            stencil(1, u1, m1, d1, k, put_f)
        send_chunk(c)
    for h in halo:
        h.wait_recv()
    mix(w0, u0, m0, 0, 1)
    mix(w0, u0, m0, T + 1, T + 2)
    for k in (0, 1, T, T + 1):
        stencil(0, u0, m0, d0, k, put_u1)
    mix(w1, u1, m1, 0, 2)
    mix(w1, u1, m1, T, T + 2)
    for c in range(len(chunks) - 2, len(chunks)):
        for k in range(*chunks[c]):
            stencil(1, u1, m1, d1, k, put_f)
        send_chunk(c)

    def weight(k):
        return 0.5 + mask_ref[0:1, tl(k - 1)].astype(f32)

    def sq(k, other):
        dd = fall[me, :, tl(k - 1)].astype(f32) - other
        return jnp.sum(dd * dd, axis=0, keepdims=True) * weight(k)

    tru.wait()
    err = jnp.zeros((1, L), f32)
    for k in range(1, T + 1):
        err = err + sq(k, truth[:, tl(k - 1)].astype(f32))

    dist = {j: jnp.zeros((1, L), f32) for j in range(M - 1)}
    order = []
    for j in range(1, C):
        order.append(lax.rem(chip + j, C) * 2 + core)
    order.append(partner)
    for j in range(1, C):
        order.append(lax.rem(chip + j, C) * 2 + (1 - core))

    def add_dist(i, c):
        acc = dist[i]
        for k in range(*chunks[c]):
            acc = acc + sq(k, fall[order[i], :, tl(k - 1)].astype(f32))
        dist[i] = acc

    for c in range(len(chunks)):
        for i in range(C - 1):
            wait_chunk(order[i], c)
            x = rc(fall.at[order[i], :, csl(c)], fall.at[order[i], :, csl(c)], fsr.at[i, c],
                   fr.at[order[i], c], dev(sp, partner))
            x.start()
            sends.append(x)
        wait_chunk(order[C - 1], c)
        for i in range(C):
            add_dist(i, c)
    for c in range(len(chunks)):
        for i in range(C, M - 1):
            wait_chunk(order[i], c)
            add_dist(i, c)

    scale = 1.0 / (V * N) / (2.0 * gaussian_radius)
    we = jnp.exp(-jnp.sum(err, axis=1, keepdims=True) * scale)
    wk = [jnp.exp(-jnp.sum(dist[i], axis=1, keepdims=True) * scale) * (1.0 / M) for i in range(M - 1)]
    wsum = wk[0]
    for x in wk[1:]:
        wsum = wsum + x

    def terms(l, gp, m, k):
        nb = nbrs(m, k)
        t = [jnp.sum(gp * x, axis=0, keepdims=True) for x in nb]
        t = jnp.concatenate([t[0], t[1], t[2], t[3] * um, t[4] * lm], axis=0)
        ctb[l, me, :, tl(k - 1)] = t.astype(bf16)

    def adjoint(k):
        f = fall[me, :, tl(k - 1)].astype(f32)
        g = we * (f - truth[:, tl(k - 1)].astype(f32))
        for i in range(M - 1):
            g = g - wk[i] * (f - fall[order[i], :, tl(k - 1)].astype(f32))
        g1[:, tl(k)] = g
        gp = g * d1[:, tl(k)]
        gp1[:, tl(k)] = gp
        return g, gp

    def local_sum(c, gp):
        return c[0] * gp + pltpu.roll(c[3] * gp, 1, 1) + pltpu.roll(c[4] * gp, L - 1, 1)

    g, gp = adjoint(1)
    c = coef(1, 1)
    part = local_sum(c, gp) + roll64(c[2] * gp)
    pk_out[0, 0] = jnp.where(hi_lane, roll64(part), c[2] * gp).astype(bf16)
    pk_out[0, 1] = g.astype(bf16)
    pk_l = rc(pk_out.at[0], pk_in.at[1], ps.at[0], pr.at[1], dev(left, me))
    pk_l.start()
    g, gp = adjoint(T)
    c = coef(1, T)
    part = local_sum(c, gp) + roll64(c[1] * gp)
    pk_out[1, 0] = jnp.where(hi_lane, c[1] * gp, roll64(part)).astype(bf16)
    pk_out[1, 1] = g.astype(bf16)
    pk_r = rc(pk_out.at[1], pk_in.at[0], ps.at[1], pr.at[0], dev(right, me))
    pk_r.start()
    for k in range(2, T):
        adjoint(k)

    def send_terms(l):
        for j in range(1, M):
            x = rc(ctb.at[l, me], ctb.at[l, me], cs.at[l, j], cr.at[l, me], dev(sp, lax.rem(me + j, M)))
            x.start()
            sends.append(x)

    for k in range(1, T + 1):
        terms(1, gp1[:, tl(k)], m1, k)
    send_terms(1)

    def back(l, gp_ref, gm, k, west, east):
        c = coef(l, k)
        gpk = gp_ref[:, tl(k)]
        if west is None:
            west = coef(l, k - 1)[1] * gp_ref[:, tl(k - 1)]
        if east is None:
            east = coef(l, k + 1)[2] * gp_ref[:, tl(k + 1)]
        s = local_sum(c, gpk) + roll64(jnp.where(hi_lane, west, c[1] * gpk))
        s = s + roll64(jnp.where(hi_lane, c[2] * gpk, east))
        gm[:, tl(k)] = s.astype(bf16)

    def mixt(w, src, k0, k1, put):
        for k in range(k0, k1, 2):
            n = min(k + 2, k1) - k
            r = lax.dot_general(w, src[:, pl.ds(k * L, n * L)], (((0,), (0,)), ((), ())),
                                preferred_element_type=f32)
            for i in range(n):
                put(k + i, r[:, i * L : (i + 1) * L])

    def put_gp0(k, r):
        gm = g1[:, tl(k)] + r
        g1[:, tl(k)] = gm
        gp0[:, tl(k)] = gm * d0[:, tl(k)]

    for k in range(2, T):
        back(1, gp1, gm1, k, None, None)
    mixt(w1, gm1, 2, T, put_gp0)

    pk_l.wait_recv()
    pk_r.wait_recv()
    pl0 = pk_in[0, 0].astype(f32)
    pr0 = pk_in[1, 0].astype(f32)
    g1[:, tl(0)] = pk_in[0, 1].astype(f32)
    g1[:, tl(T + 1)] = pk_in[1, 1].astype(f32)
    gm1[:, tl(0)] = roll64(pl0 + coef(1, 1)[2] * gp1[:, tl(1)]).astype(bf16)
    gm1[:, tl(T + 1)] = roll64(pr0 + coef(1, T)[1] * gp1[:, tl(T)]).astype(bf16)
    back(1, gp1, gm1, 1, pl0, None)
    back(1, gp1, gm1, T, None, pr0)
    mixt(w1, gm1, 0, 2, put_gp0)
    mixt(w1, gm1, T, T + 2, put_gp0)

    for k in range(1, T + 1):
        terms(0, gp0[:, tl(k)], m0, k)
    send_terms(0)

    def put_out(k, r):
        out_ref[0, :, tl(k - 1)] = g1[:, tl(k)] + r

    for k in range(1, T + 1):
        back(0, gp0, gm0, k, None, None)
    mixt(w0, gm0, 1, T + 1, put_out)

    for l in (1, 0):
        for j in range(1, M):
            src = lax.rem(me + j, M)
            rc(ctb.at[l, src], ctb.at[l, src], cs.at[l, j], cr.at[l, src], dev(sp, src)).wait_recv()
        tot = ctb[l, 0].astype(f32)
        for j in range(1, M):
            tot = tot + ctb[l, j].astype(f32)
        cg_ref[l] = tot * (1.0 / M)

    for h in halo:
        h.wait_send()
    pk_l.wait_send()
    pk_r.wait_send()
    for x in sends:
        x.wait_send()


def per_device(S, M, latent, verifying_truth, mix_weight, coefficients, land_mask):
    _, V, N = latent.shape
    T = N // L
    E = N + 2 * L
    nc = len(chunk_plan(T))
    dma = pltpu.SemaphoreType.DMA
    vm = pltpu.VMEM
    anyspec = pl.BlockSpec(memory_space=pl.ANY)
    vspec = pl.BlockSpec(memory_space=pltpu.VMEM)
    return pl.pallas_call(
        functools.partial(kernel, S, M, T),
        out_shape=(jax.ShapeDtypeStruct((1, V, N), f32), jax.ShapeDtypeStruct((2, 5, N), f32)),
        in_specs=[anyspec, anyspec, vspec, vspec, vspec],
        out_specs=(vspec, vspec),
        scratch_shapes=[
            vm((V, E), bf16), vm((V, E), f32), vm((V, E), f32),
            vm((V, E), bf16), vm((V, E), f32), vm((V, E), f32),
            vm((M, V, N), bf16), vm((V, N), bf16), vm((2, 5, L), f32),
            vm((V, E), f32), vm((V, E), f32), vm((V, E), bf16),
            vm((V, E), f32), vm((V, E), bf16),
            vm((2, 2, V, L), bf16), vm((2, 2, V, L), bf16), vm((2, M, 5, N), bf16),
            dma((2,)), dma((4,)), dma((4,)), dma((2,)), dma((2,)),
            dma((M // 2, nc)), dma((nc,)), dma((M // 2, nc)), dma((M, nc)),
            dma((2, M)), dma((2, M)),
        ],
        compiler_params=pltpu.CompilerParams(collective_id=0, has_side_effects=True,
                                             vmem_limit_bytes=48 * 1024 * 1024),
    )(latent, verifying_truth, mix_weight, coefficients, land_mask.reshape(1, N))


def solution(mesh):
    in_specs = (
        P("members", None, "space"),
        P(None, "space"),
        P(),
        P(None, None, "space"),
        P("space"),
    )
    out_specs = (P("members", None, "space"), P(None, None, "space"))
    return jax.shard_map(
        functools.partial(per_device, mesh.shape["space"], mesh.shape["members"]),
        mesh=mesh, in_specs=in_specs, out_specs=out_specs, check_vma=False
    )
```

```python
import functools

import jax
import jax.numpy as jnp
from jax import lax
from jax.experimental import pallas as pl
from jax.experimental.pallas import tpu as pltpu
from jax.sharding import PartitionSpec as P

LAT = 64
L = 128
gaussian_radius = 4.0
MESH = pl.DeviceIdType.MESH
f32 = jnp.float32
bf16 = jnp.bfloat16


def chunk_plan(T):
    lo, hi = 3, T - 1
    parts = []
    n = hi - lo
    if n > 0:
        pieces = 3
        edges = [lo + n * i // pieces for i in range(pieces + 1)]
        parts = [(a, b) for a, b in zip(edges[:-1], edges[1:]) if b > a]
    parts += [(1, 3), (T - 1, T + 1)]
    return parts


def kernel(
    S, M, T,
    lat_hbm, truth_hbm, w_hbm, c_hbm, mask_hbm,
    out_ref, cg_ref,
    u0, m0, d0, u1, m1, d1, fall, truth, ch,
    gp1, g1, gm1, gp0, gm0, pk_out, pk_in, ctb, w_ref, c_ref, mask_ref, og,
    ls, hs, hr, ps, pr, fsx, fsp, fsr, fr, cs, cr, cs0, cr0,
):
    V = u0.shape[0]
    N = T * L
    C = M // 2
    chunks = chunk_plan(T)
    sp = lax.axis_index("space")
    me = lax.axis_index("members")
    right, left = lax.rem(sp + 1, S), lax.rem(sp + S - 1, S)
    core = lax.rem(me, 2)
    chip = me // 2
    partner = chip * 2 + (1 - core)

    def dev(s, m):
        return {"space": s, "members": m}

    def tl(k):
        return pl.ds(k * L, L)

    def rc(src, dst, a, b, d):
        return pltpu.make_async_remote_copy(
            src_ref=src, dst_ref=dst, send_sem=a, recv_sem=b,
            device_id=d, device_id_type=MESH)

    barrier = pltpu.get_barrier_semaphore()
    for s in (left, right):
        pl.semaphore_signal(barrier, inc=1, device_id=dev(s, me), device_id_type=MESH)
    for j in range(1, M):
        pl.semaphore_signal(barrier, inc=1, device_id=dev(sp, lax.rem(me + j, M)), device_id_type=MESH)
    own = pltpu.make_async_copy(lat_hbm.at[0], u0.at[:, pl.ds(L, N)], ls.at[0])
    own.start()
    tru = pltpu.make_async_copy(truth_hbm, truth, ls.at[1])
    tru.start()
    cin = pltpu.make_async_copy(c_hbm, c_ref, ls.at[2])
    cin.start()
    win = pltpu.make_async_copy(w_hbm, w_ref, ls.at[3])
    win.start()
    min_ = pltpu.make_async_copy(mask_hbm, mask_ref, ls.at[4])
    min_.start()

    halo = [
        rc(lat_hbm.at[0, :, pl.ds(N - L, L)], u0.at[:, pl.ds(0, L)], hs.at[0], hr.at[0], dev(right, me)),
        rc(lat_hbm.at[0, :, pl.ds(0, L)], u0.at[:, pl.ds(N + L, L)], hs.at[1], hr.at[1], dev(left, me)),
        rc(c_hbm.at[:, :, pl.ds(N - L, L)], ch.at[0], hs.at[2], hr.at[2], dev(right, me)),
        rc(c_hbm.at[:, :, pl.ds(0, L)], ch.at[1], hs.at[3], hr.at[3], dev(left, me)),
    ]
    lane = lax.broadcasted_iota(jnp.int32, (1, L), 1)
    lat_i = lax.rem(lane, LAT)
    um = (lat_i < LAT - 1).astype(f32)
    lm = (lat_i >= 1).astype(f32)
    hi_lane = lax.broadcasted_iota(jnp.int32, (V, L), 1) >= LAT

    def coef(l, k):
        if k == 0:
            c = [ch[0, j, 0:1, :] for j in range(5)]
        elif k == T + 1:
            c = [ch[1, j, 0:1, :] for j in range(5)]
        else:
            c = [c_ref[j, l : l + 1, tl(k - 1)] for j in range(5)]
        c[3] = c[3] * um
        c[4] = c[4] * lm
        return c

    def roll64(x):
        return pltpu.roll(x, LAT, 1)

    def nbrs(m, k):
        mk = m[:, tl(k)]
        mp = m[:, tl(max(k - 1, 0))]
        mn = m[:, tl(min(k + 1, T + 1))]
        return (mk, roll64(jnp.where(hi_lane, mk, mn)), roll64(jnp.where(hi_lane, mp, mk)),
                pltpu.roll(mk, L - 1, 1), pltpu.roll(mk, 1, 1))

    win.wait()
    wv = w_ref[...].astype(f32)
    w0 = wv[:, 0, :].astype(bf16)
    w1 = wv[:, 1, :].astype(bf16)

    def mix(w, src, dst, k0, k1):
        for k in range(k0, k1, 2):
            sl = pl.ds(k * L, (min(k + 2, k1) - k) * L)
            dst[:, sl] = jnp.dot(w, src[:, sl], preferred_element_type=f32).astype(bf16).astype(f32)

    def stencil(l, u, m, d, k, put):
        nb = nbrs(m, k)
        c = coef(l, k)
        pre = c[0] * nb[0]
        for j in range(1, 5):
            pre = pre + c[j] * nb[j]
        s = jnp.tanh(pre)
        put(k, (u[:, tl(k)].astype(f32) + s).astype(bf16))
        d[:, tl(k)] = 1.0 - s * s

    def put_u1(k, v):
        u1[:, tl(k)] = v

    def put_f(k, v):
        fall[me, :, tl(k - 1)] = v

    def csl(c):
        a, b = chunks[c]
        return pl.ds((a - 1) * L, (b - a) * L)

    sends = []

    def send_chunk(c):
        for j in range(1, C):
            to = lax.rem(chip + j, C) * 2 + core
            x = rc(fall.at[me, :, csl(c)], fall.at[me, :, csl(c)], fsx.at[j, c], fr.at[me, c], dev(sp, to))
            x.start()
            sends.append(x)
        x = rc(fall.at[me, :, csl(c)], fall.at[me, :, csl(c)], fsp.at[c], fr.at[me, c], dev(sp, partner))
        x.start()
        sends.append(x)

    def wait_chunk(src, c):
        rc(fall.at[src, :, csl(c)], fall.at[src, :, csl(c)], fsp.at[c], fr.at[src, c], dev(sp, partner)).wait_recv()

    own.wait()
    cin.wait()
    front = {"m0": 1, "u1": 2, "m1": 2}
    ni = len(chunks) - 2
    for c in range(ni):
        lo, hi = chunks[c]
        to = min(T + 1, hi + 2)
        mix(w0, u0, m0, front["m0"], to)
        front["m0"] = to
        to = min(T, hi + 1)
        for k in range(front["u1"], to):
            stencil(0, u0, m0, d0, k, put_u1)
        mix(w1, u1, m1, front["m1"], to)
        front["u1"] = front["m1"] = to
        for k in range(lo, hi):
            stencil(1, u1, m1, d1, k, put_f)
        if c == 0:
            pl.semaphore_wait(barrier, M + 1)
            for h in halo:
                h.start()
        send_chunk(c)

    def edges():
        for h in halo:
            h.wait_recv()
        mix(w0, u0, m0, 0, 1)
        mix(w0, u0, m0, T + 1, T + 2)
        for k in (0, 1, T, T + 1):
            stencil(0, u0, m0, d0, k, put_u1)
        mix(w1, u1, m1, 0, 2)
        mix(w1, u1, m1, T, T + 2)
        for c in range(ni, len(chunks)):
            for k in range(*chunks[c]):
                stencil(1, u1, m1, d1, k, put_f)
            send_chunk(c)

    def weight(k):
        return 0.5 + mask_ref[tl(k - 1)].astype(f32).reshape(1, L)

    def sq(k, other):
        dd = fall[me, :, tl(k - 1)].astype(f32) - other
        return jnp.sum(dd * dd, axis=0, keepdims=True) * weight(k)

    tru.wait()
    min_.wait()
    errs = [jnp.zeros((1, L), f32)]

    def add_err(c):
        for k in range(*chunks[c]):
            errs[0] = errs[0] + sq(k, truth[:, tl(k - 1)].astype(f32))

    for c in range(ni):
        add_err(c)

    dist = {j: jnp.zeros((1, L), f32) for j in range(M - 1)}
    order = []
    for j in range(1, C):
        order.append(lax.rem(chip + j, C) * 2 + core)
    order.append(partner)
    for j in range(1, C):
        order.append(lax.rem(chip + j, C) * 2 + (1 - core))

    def add_dist(i, c):
        acc = dist[i]
        for k in range(*chunks[c]):
            acc = acc + sq(k, fall[order[i], :, tl(k - 1)].astype(f32))
        dist[i] = acc

    for c in range(len(chunks)):
        if c == min(2, ni):
            edges()
            add_err(ni)
            add_err(ni + 1)
        for i in range(C - 1):
            wait_chunk(order[i], c)
            x = rc(fall.at[order[i], :, csl(c)], fall.at[order[i], :, csl(c)], fsr.at[i, c],
                   fr.at[order[i], c], dev(sp, partner))
            x.start()
            sends.append(x)
        wait_chunk(order[C - 1], c)
        for i in range(C):
            add_dist(i, c)
    for c in range(len(chunks)):
        for i in range(C, M - 1):
            wait_chunk(order[i], c)
            add_dist(i, c)

    scale = 1.0 / (V * N) / (2.0 * gaussian_radius)
    we = jnp.exp(-jnp.sum(errs[0], axis=1, keepdims=True) * scale)
    wk = [jnp.exp(-jnp.sum(dist[i], axis=1, keepdims=True) * scale) * (1.0 / M) for i in range(M - 1)]
    wsum = wk[0]
    for x in wk[1:]:
        wsum = wsum + x

    def terms(l, gp, m, k):
        nb = nbrs(m, k)
        t = [jnp.sum(gp * x, axis=0, keepdims=True) for x in nb]
        t = jnp.concatenate([t[0], t[1], t[2], t[3] * um, t[4] * lm], axis=0)
        ctb[l, me, :, tl(k - 1)] = t.astype(bf16)

    def adjoint(k):
        f = fall[me, :, tl(k - 1)].astype(f32)
        g = we * (f - truth[:, tl(k - 1)].astype(f32))
        for i in range(M - 1):
            g = g - wk[i] * (f - fall[order[i], :, tl(k - 1)].astype(f32))
        g1[:, tl(k)] = g
        gp = g * d1[:, tl(k)]
        gp1[:, tl(k)] = gp
        return g, gp

    def local_sum(c, gp):
        return c[0] * gp + pltpu.roll(c[3] * gp, 1, 1) + pltpu.roll(c[4] * gp, L - 1, 1)

    g, gp = adjoint(1)
    c = coef(1, 1)
    part = local_sum(c, gp) + roll64(c[2] * gp)
    pk_out[0, 0] = jnp.where(hi_lane, roll64(part), c[2] * gp).astype(bf16)
    pk_out[0, 1] = g.astype(bf16)
    pk_l = rc(pk_out.at[0], pk_in.at[1], ps.at[0], pr.at[1], dev(left, me))
    pk_l.start()
    g, gp = adjoint(T)
    c = coef(1, T)
    part = local_sum(c, gp) + roll64(c[1] * gp)
    pk_out[1, 0] = jnp.where(hi_lane, c[1] * gp, roll64(part)).astype(bf16)
    pk_out[1, 1] = g.astype(bf16)
    pk_r = rc(pk_out.at[1], pk_in.at[0], ps.at[1], pr.at[0], dev(right, me))
    pk_r.start()
    for k in range(2, T):
        adjoint(k)

    def send_terms():
        for j in range(1, M):
            x = rc(ctb.at[1, me], ctb.at[1, me], cs.at[j], cr.at[me], dev(sp, lax.rem(me + j, M)))
            x.start()
            sends.append(x)

    for k in range(1, T + 1):
        terms(1, gp1[:, tl(k)], m1, k)
    send_terms()

    def back(l, gp_ref, gm, k, west, east):
        c = coef(l, k)
        gpk = gp_ref[:, tl(k)]
        if west is None:
            west = coef(l, k - 1)[1] * gp_ref[:, tl(k - 1)]
        if east is None:
            east = coef(l, k + 1)[2] * gp_ref[:, tl(k + 1)]
        s = local_sum(c, gpk) + roll64(jnp.where(hi_lane, west, c[1] * gpk))
        s = s + roll64(jnp.where(hi_lane, c[2] * gpk, east))
        gm[:, tl(k)] = s.astype(bf16)

    def mixt(w, src, k0, k1, put):
        for k in range(k0, k1, 2):
            n = min(k + 2, k1) - k
            r = lax.dot_general(w, src[:, pl.ds(k * L, n * L)], (((0,), (0,)), ((), ())),
                                preferred_element_type=f32)
            for i in range(n):
                put(k + i, r[:, i * L : (i + 1) * L])

    def put_gp0(k, r):
        gm = g1[:, tl(k)] + r
        g1[:, tl(k)] = gm
        gp0[:, tl(k)] = gm * d0[:, tl(k)]

    for k in range(2, T):
        back(1, gp1, gm1, k, None, None)
    mixt(w1, gm1, 2, T, put_gp0)

    def put_out(k, r):
        og[:, tl(k - 1)] = g1[:, tl(k)] + r

    pieces = [(2, T), (1, 2), (T, T + 1)]

    def psl(p):
        a, b = pieces[p]
        return pl.ds((a - 1) * L, (b - a) * L)

    def send_piece(p):
        for j in range(1, M):
            x = rc(ctb.at[0, me, :, psl(p)], ctb.at[0, me, :, psl(p)], cs0.at[p, j], cr0.at[p, me],
                   dev(sp, lax.rem(me + j, M)))
            x.start()
            sends.append(x)

    for k in range(2, T):
        terms(0, gp0[:, tl(k)], m0, k)
    send_piece(0)
    for k in range(3, T - 1):
        back(0, gp0, gm0, k, None, None)
    mixt(w0, gm0, 3, T - 1, put_out)
    outs = []

    def put_rows(a, b):
        sl = pl.ds((a - 1) * L, (b - a) * L)
        x = pltpu.make_async_copy(og.at[:, sl], out_ref.at[:, 0, sl], ls.at[5 + len(outs)])
        x.start()
        outs.append(x)

    put_rows(3, T - 1)

    pk_l.wait_recv()
    pk_r.wait_recv()
    pl0 = pk_in[0, 0].astype(f32)
    pr0 = pk_in[1, 0].astype(f32)
    g1[:, tl(0)] = pk_in[0, 1].astype(f32)
    g1[:, tl(T + 1)] = pk_in[1, 1].astype(f32)
    gm1[:, tl(0)] = roll64(pl0 + coef(1, 1)[2] * gp1[:, tl(1)]).astype(bf16)
    gm1[:, tl(T + 1)] = roll64(pr0 + coef(1, T)[1] * gp1[:, tl(T)]).astype(bf16)
    back(1, gp1, gm1, 1, pl0, None)
    back(1, gp1, gm1, T, None, pr0)
    mixt(w1, gm1, 0, 2, put_gp0)
    mixt(w1, gm1, T, T + 2, put_gp0)
    terms(0, gp0[:, tl(1)], m0, 1)
    send_piece(1)
    terms(0, gp0[:, tl(T)], m0, T)
    send_piece(2)
    for k in (1, 2, T - 1, T):
        back(0, gp0, gm0, k, None, None)
    mixt(w0, gm0, 1, 3, put_out)
    put_rows(1, 3)
    mixt(w0, gm0, T - 1, T + 1, put_out)
    put_rows(T - 1, T + 1)

    for l in (1, 0):
        for j in range(1, M):
            src = lax.rem(me + j, M)
            if l == 1:
                rc(ctb.at[l, src], ctb.at[l, src], cs.at[j], cr.at[src], dev(sp, src)).wait_recv()
            else:
                for p in range(3):
                    rc(ctb.at[0, src, :, psl(p)], ctb.at[0, src, :, psl(p)], cs0.at[p, j], cr0.at[p, src],
                       dev(sp, src)).wait_recv()
        tot = ctb[l, 0].astype(f32)
        for j in range(1, M):
            tot = tot + ctb[l, j].astype(f32)
        cg_ref[:, l, :] = tot * (1.0 / M)

    for x in outs:
        x.wait()
    for h in halo:
        h.wait_send()
    pk_l.wait_send()
    pk_r.wait_send()
    for x in sends:
        x.wait_send()


def per_device(S, M, latent, verifying_truth, mix_weight, coefficients, land_mask):
    _, V, N = latent.shape
    T = N // L
    E = N + 2 * L
    nc = len(chunk_plan(T))
    dma = pltpu.SemaphoreType.DMA
    vm = pltpu.VMEM
    anyspec = pl.BlockSpec(memory_space=pltpu.HBM)
    vspec = pl.BlockSpec(memory_space=pltpu.VMEM)
    grad, cg = pl.pallas_call(
        functools.partial(kernel, S, M, T),
        out_shape=(jax.ShapeDtypeStruct((V, 1, N), f32), jax.ShapeDtypeStruct((5, 2, N), f32)),
        in_specs=[anyspec] * 5,
        out_specs=(anyspec, vspec),
        scratch_shapes=[
            vm((V, E), bf16), vm((V, E), f32), vm((V, E), f32),
            vm((V, E), bf16), vm((V, E), f32), vm((V, E), f32),
            vm((M, V, N), bf16), vm((V, N), bf16), vm((2, 5, 2, L), f32),
            vm((V, E), f32), vm((V, E), f32), vm((V, E), bf16),
            vm((V, E), f32), vm((V, E), bf16),
            vm((2, 2, V, L), bf16), vm((2, 2, V, L), bf16), vm((2, M, 5, N), bf16),
            vm((V, 2, V), bf16), vm((5, 2, N), f32), vm((N,), jnp.int32), vm((V, N), f32),
            dma((8,)), dma((4,)), dma((4,)), dma((2,)), dma((2,)),
            dma((M // 2, nc)), dma((nc,)), dma((M // 2, nc)), dma((M, nc)),
            dma((M,)), dma((M,)), dma((3, M)), dma((3, M)),
        ],
        compiler_params=pltpu.CompilerParams(collective_id=0, has_side_effects=True),
    )(latent, verifying_truth, jnp.transpose(mix_weight, (1, 0, 2)), jnp.transpose(coefficients, (1, 0, 2)), land_mask)
    return jnp.transpose(grad, (1, 0, 2)), jnp.transpose(cg, (1, 0, 2))


def solution(mesh):
    in_specs = (
        P("members", None, "space"),
        P(None, "space"),
        P(),
        P(None, None, "space"),
        P("space"),
    )
    out_specs = (P("members", None, "space"), P(None, None, "space"))
    return jax.shard_map(
        functools.partial(per_device, mesh.shape["space"], mesh.shape["members"]),
        mesh=mesh, in_specs=in_specs, out_specs=out_specs, check_vma=False
    )
```

```python
import functools

import jax
import jax.numpy as jnp
from jax import lax
from jax.experimental import pallas as pl
from jax.experimental.pallas import tpu as pltpu
from jax.sharding import PartitionSpec as P

LAT = 64
L = 128
gaussian_radius = 4.0
MESH = pl.DeviceIdType.MESH
f32 = jnp.float32
bf16 = jnp.bfloat16


def chunk_plan(T):
    lo, hi = 3, T - 1
    parts = []
    n = hi - lo
    if n > 0:
        pieces = 3
        edges = [lo + n * i // pieces for i in range(pieces + 1)]
        parts = [(a, b) for a, b in zip(edges[:-1], edges[1:]) if b > a]
    parts += [(1, 3), (T - 1, T + 1)]
    return parts


def kernel(
    S, M, T,
    lat_hbm, truth_hbm, w_hbm, c_hbm, mask_hbm,
    out_ref, cg_ref,
    u0, m0, d0, u1, m1, d1, fall, truth, ch,
    gp1, g1, gm1, gp0, gm0, pk_out, pk_in, ctb, w_ref, c_ref, mask_ref,
    ls, hs, hr, ps, pr, fsx, fsp, fsr, fr, cs, cr, cs0, cr0,
):
    V = u0.shape[0]
    N = T * L
    C = M // 2
    chunks = chunk_plan(T)
    sp = lax.axis_index("space")
    me = lax.axis_index("members")
    right, left = lax.rem(sp + 1, S), lax.rem(sp + S - 1, S)
    core = lax.rem(me, 2)
    chip = me // 2
    partner = chip * 2 + (1 - core)

    def dev(s, m):
        return {"space": s, "members": m}

    def tl(k):
        return pl.ds(k * L, L)

    def rc(src, dst, a, b, d):
        return pltpu.make_async_remote_copy(
            src_ref=src, dst_ref=dst, send_sem=a, recv_sem=b,
            device_id=d, device_id_type=MESH)

    barrier = pltpu.get_barrier_semaphore()
    for s in (left, right):
        pl.semaphore_signal(barrier, inc=1, device_id=dev(s, me), device_id_type=MESH)
    for j in range(1, M):
        pl.semaphore_signal(barrier, inc=1, device_id=dev(sp, lax.rem(me + j, M)), device_id_type=MESH)
    own = pltpu.make_async_copy(lat_hbm.at[0], u0.at[:, pl.ds(L, N)], ls.at[0])
    own.start()
    tru = pltpu.make_async_copy(truth_hbm, truth, ls.at[1])
    tru.start()
    cin = pltpu.make_async_copy(c_hbm, c_ref, ls.at[2])
    cin.start()
    win = pltpu.make_async_copy(w_hbm, w_ref, ls.at[3])
    win.start()
    min_ = pltpu.make_async_copy(mask_hbm, mask_ref, ls.at[4])
    min_.start()

    halo = [
        rc(lat_hbm.at[0, :, pl.ds(N - L, L)], u0.at[:, pl.ds(0, L)], hs.at[0], hr.at[0], dev(right, me)),
        rc(lat_hbm.at[0, :, pl.ds(0, L)], u0.at[:, pl.ds(N + L, L)], hs.at[1], hr.at[1], dev(left, me)),
        rc(c_hbm.at[:, :, pl.ds(N - L, L)], ch.at[0], hs.at[2], hr.at[2], dev(right, me)),
        rc(c_hbm.at[:, :, pl.ds(0, L)], ch.at[1], hs.at[3], hr.at[3], dev(left, me)),
    ]
    lane = lax.broadcasted_iota(jnp.int32, (1, L), 1)
    lat_i = lax.rem(lane, LAT)
    um = (lat_i < LAT - 1).astype(f32)
    lm = (lat_i >= 1).astype(f32)
    hi_lane = lax.broadcasted_iota(jnp.int32, (V, L), 1) >= LAT

    def coef(l, k):
        if k == 0:
            c = [ch[0, j, 0:1, :] for j in range(5)]
        elif k == T + 1:
            c = [ch[1, j, 0:1, :] for j in range(5)]
        else:
            c = [c_ref[j, l : l + 1, tl(k - 1)] for j in range(5)]
        c[3] = c[3] * um
        c[4] = c[4] * lm
        return c

    def roll64(x):
        return pltpu.roll(x, LAT, 1)

    def nbrs(m, k):
        mk = m[:, tl(k)]
        mp = m[:, tl(max(k - 1, 0))]
        mn = m[:, tl(min(k + 1, T + 1))]
        return (mk, roll64(jnp.where(hi_lane, mk, mn)), roll64(jnp.where(hi_lane, mp, mk)),
                pltpu.roll(mk, L - 1, 1), pltpu.roll(mk, 1, 1))

    win.wait()
    wv = w_ref[...].astype(f32)
    w0 = wv[:, 0, :].astype(bf16)
    w1 = wv[:, 1, :].astype(bf16)

    def mix(w, src, dst, k0, k1):
        for k in range(k0, k1, 2):
            sl = pl.ds(k * L, (min(k + 2, k1) - k) * L)
            dst[:, sl] = jnp.dot(w, src[:, sl], preferred_element_type=f32).astype(bf16).astype(f32)

    def stencil(l, u, m, d, k, put):
        nb = nbrs(m, k)
        c = coef(l, k)
        pre = c[0] * nb[0]
        for j in range(1, 5):
            pre = pre + c[j] * nb[j]
        s = jnp.tanh(pre)
        put(k, (u[:, tl(k)].astype(f32) + s).astype(bf16))
        d[:, tl(k)] = 1.0 - s * s

    def put_u1(k, v):
        u1[:, tl(k)] = v

    def put_f(k, v):
        fall[me, :, tl(k - 1)] = v

    def csl(c):
        a, b = chunks[c]
        return pl.ds((a - 1) * L, (b - a) * L)

    sends = []

    def send_chunk(c):
        for j in range(1, C):
            to = lax.rem(chip + j, C) * 2 + core
            x = rc(fall.at[me, :, csl(c)], fall.at[me, :, csl(c)], fsx.at[j, c], fr.at[me, c], dev(sp, to))
            x.start()
            sends.append(x)
        x = rc(fall.at[me, :, csl(c)], fall.at[me, :, csl(c)], fsp.at[c], fr.at[me, c], dev(sp, partner))
        x.start()
        sends.append(x)

    def wait_chunk(src, c):
        rc(fall.at[src, :, csl(c)], fall.at[src, :, csl(c)], fsp.at[c], fr.at[src, c], dev(sp, partner)).wait_recv()

    own.wait()
    cin.wait()
    front = {"m0": 1, "u1": 2, "m1": 2}
    ni = len(chunks) - 2
    for c in range(ni):
        lo, hi = chunks[c]
        to = min(T + 1, hi + 2)
        mix(w0, u0, m0, front["m0"], to)
        front["m0"] = to
        to = min(T, hi + 1)
        for k in range(front["u1"], to):
            stencil(0, u0, m0, d0, k, put_u1)
        mix(w1, u1, m1, front["m1"], to)
        front["u1"] = front["m1"] = to
        for k in range(lo, hi):
            stencil(1, u1, m1, d1, k, put_f)
        if c == 0:
            pl.semaphore_wait(barrier, M + 1)
            for h in halo:
                h.start()
        send_chunk(c)

    def edges():
        for h in halo:
            h.wait_recv()
        mix(w0, u0, m0, 0, 1)
        mix(w0, u0, m0, T + 1, T + 2)
        for k in (0, 1, T, T + 1):
            stencil(0, u0, m0, d0, k, put_u1)
        mix(w1, u1, m1, 0, 2)
        mix(w1, u1, m1, T, T + 2)
        for c in range(ni, len(chunks)):
            for k in range(*chunks[c]):
                stencil(1, u1, m1, d1, k, put_f)
            send_chunk(c)

    def weight(k):
        return 0.5 + mask_ref[tl(k - 1)].astype(f32).reshape(1, L)

    def sq(k, other):
        dd = fall[me, :, tl(k - 1)].astype(f32) - other
        return jnp.sum(dd * dd, axis=0, keepdims=True) * weight(k)

    tru.wait()
    min_.wait()
    errs = [jnp.zeros((1, L), f32)]

    def add_err(c):
        for k in range(*chunks[c]):
            errs[0] = errs[0] + sq(k, truth[:, tl(k - 1)].astype(f32))

    for c in range(ni):
        add_err(c)

    dist = {j: jnp.zeros((1, L), f32) for j in range(M - 1)}
    order = []
    for j in range(1, C):
        order.append(lax.rem(chip + j, C) * 2 + core)
    order.append(partner)
    for j in range(1, C):
        order.append(lax.rem(chip + j, C) * 2 + (1 - core))

    def add_dist(i, c):
        acc = dist[i]
        for k in range(*chunks[c]):
            acc = acc + sq(k, fall[order[i], :, tl(k - 1)].astype(f32))
        dist[i] = acc

    for c in range(len(chunks)):
        if c == min(2, ni):
            edges()
            add_err(ni)
            add_err(ni + 1)
        for i in range(C - 1):
            wait_chunk(order[i], c)
            x = rc(fall.at[order[i], :, csl(c)], fall.at[order[i], :, csl(c)], fsr.at[i, c],
                   fr.at[order[i], c], dev(sp, partner))
            x.start()
            sends.append(x)
        wait_chunk(order[C - 1], c)
        for i in range(C):
            add_dist(i, c)
    for c in range(len(chunks)):
        for i in range(C, M - 1):
            wait_chunk(order[i], c)
            add_dist(i, c)

    scale = 1.0 / (V * N) / (2.0 * gaussian_radius)
    we = jnp.exp(-jnp.sum(errs[0], axis=1, keepdims=True) * scale)
    wk = [jnp.exp(-jnp.sum(dist[i], axis=1, keepdims=True) * scale) * (1.0 / M) for i in range(M - 1)]
    wsum = wk[0]
    for x in wk[1:]:
        wsum = wsum + x

    def terms(l, gp, m, k):
        nb = nbrs(m, k)
        t = [jnp.sum(gp * x, axis=0, keepdims=True) for x in nb]
        t = jnp.concatenate([t[0], t[1], t[2], t[3] * um, t[4] * lm], axis=0)
        ctb[l, me, :, tl(k - 1)] = t.astype(bf16)

    def adjoint(k):
        f = fall[me, :, tl(k - 1)].astype(f32)
        g = we * (f - truth[:, tl(k - 1)].astype(f32))
        for i in range(M - 1):
            g = g - wk[i] * (f - fall[order[i], :, tl(k - 1)].astype(f32))
        g1[:, tl(k)] = g
        gp = g * d1[:, tl(k)]
        gp1[:, tl(k)] = gp
        return g, gp

    def local_sum(c, gp):
        return c[0] * gp + pltpu.roll(c[3] * gp, 1, 1) + pltpu.roll(c[4] * gp, L - 1, 1)

    g, gp = adjoint(1)
    c = coef(1, 1)
    part = local_sum(c, gp) + roll64(c[2] * gp)
    pk_out[0, 0] = jnp.where(hi_lane, roll64(part), c[2] * gp).astype(bf16)
    pk_out[0, 1] = g.astype(bf16)
    pk_l = rc(pk_out.at[0], pk_in.at[1], ps.at[0], pr.at[1], dev(left, me))
    pk_l.start()
    g, gp = adjoint(T)
    c = coef(1, T)
    part = local_sum(c, gp) + roll64(c[1] * gp)
    pk_out[1, 0] = jnp.where(hi_lane, c[1] * gp, roll64(part)).astype(bf16)
    pk_out[1, 1] = g.astype(bf16)
    pk_r = rc(pk_out.at[1], pk_in.at[0], ps.at[1], pr.at[0], dev(right, me))
    pk_r.start()
    for k in range(2, T):
        adjoint(k)

    def send_terms():
        for j in range(1, M):
            x = rc(ctb.at[1, me], ctb.at[1, me], cs.at[j], cr.at[me], dev(sp, lax.rem(me + j, M)))
            x.start()
            sends.append(x)

    for k in range(1, T + 1):
        terms(1, gp1[:, tl(k)], m1, k)
    send_terms()

    def back(l, gp_ref, gm, k, west, east):
        c = coef(l, k)
        gpk = gp_ref[:, tl(k)]
        if west is None:
            west = coef(l, k - 1)[1] * gp_ref[:, tl(k - 1)]
        if east is None:
            east = coef(l, k + 1)[2] * gp_ref[:, tl(k + 1)]
        s = local_sum(c, gpk) + roll64(jnp.where(hi_lane, west, c[1] * gpk))
        s = s + roll64(jnp.where(hi_lane, c[2] * gpk, east))
        gm[:, tl(k)] = s.astype(bf16)

    def mixt(w, src, k0, k1, put):
        for k in range(k0, k1, 2):
            n = min(k + 2, k1) - k
            r = lax.dot_general(w, src[:, pl.ds(k * L, n * L)], (((0,), (0,)), ((), ())),
                                preferred_element_type=f32)
            for i in range(n):
                put(k + i, r[:, i * L : (i + 1) * L])

    def put_gp0(k, r):
        gm = g1[:, tl(k)] + r
        g1[:, tl(k)] = gm
        gp0[:, tl(k)] = gm * d0[:, tl(k)]

    for k in range(2, T):
        back(1, gp1, gm1, k, None, None)
    mixt(w1, gm1, 2, T, put_gp0)

    def put_out(k, r):
        out_ref[:, tl(k - 1)] = g1[:, tl(k)] + r

    pieces = [(2, T), (1, 2), (T, T + 1)]

    def psl(p):
        a, b = pieces[p]
        return pl.ds((a - 1) * L, (b - a) * L)

    def send_piece(p):
        for j in range(1, M):
            x = rc(ctb.at[0, me, :, psl(p)], ctb.at[0, me, :, psl(p)], cs0.at[p, j], cr0.at[p, me],
                   dev(sp, lax.rem(me + j, M)))
            x.start()
            sends.append(x)

    for k in range(2, T):
        terms(0, gp0[:, tl(k)], m0, k)
    send_piece(0)
    for k in range(3, T - 1):
        back(0, gp0, gm0, k, None, None)
    mixt(w0, gm0, 3, T - 1, put_out)

    pk_l.wait_recv()
    pk_r.wait_recv()
    pl0 = pk_in[0, 0].astype(f32)
    pr0 = pk_in[1, 0].astype(f32)
    g1[:, tl(0)] = pk_in[0, 1].astype(f32)
    g1[:, tl(T + 1)] = pk_in[1, 1].astype(f32)
    gm1[:, tl(0)] = roll64(pl0 + coef(1, 1)[2] * gp1[:, tl(1)]).astype(bf16)
    gm1[:, tl(T + 1)] = roll64(pr0 + coef(1, T)[1] * gp1[:, tl(T)]).astype(bf16)
    back(1, gp1, gm1, 1, pl0, None)
    back(1, gp1, gm1, T, None, pr0)
    mixt(w1, gm1, 0, 2, put_gp0)
    mixt(w1, gm1, T, T + 2, put_gp0)
    terms(0, gp0[:, tl(1)], m0, 1)
    send_piece(1)
    terms(0, gp0[:, tl(T)], m0, T)
    send_piece(2)
    for k in (1, 2, T - 1, T):
        back(0, gp0, gm0, k, None, None)
    mixt(w0, gm0, 1, 3, put_out)
    mixt(w0, gm0, T - 1, T + 1, put_out)

    for l in (1, 0):
        for j in range(1, M):
            src = lax.rem(me + j, M)
            if l == 1:
                rc(ctb.at[l, src], ctb.at[l, src], cs.at[j], cr.at[src], dev(sp, src)).wait_recv()
            else:
                for p in range(3):
                    rc(ctb.at[0, src, :, psl(p)], ctb.at[0, src, :, psl(p)], cs0.at[p, j], cr0.at[p, src],
                       dev(sp, src)).wait_recv()
        tot = ctb[l, 0].astype(f32)
        for j in range(1, M):
            tot = tot + ctb[l, j].astype(f32)
        cg_ref[:, l, :] = tot * (1.0 / M)

    for h in halo:
        h.wait_send()
    pk_l.wait_send()
    pk_r.wait_send()
    for x in sends:
        x.wait_send()


def write_out(grad_ref, cg_ref, out_ref, coef_ref, sem):
    a = pltpu.make_async_copy(grad_ref, out_ref.at[:, 0, :], sem.at[0])
    b = pltpu.make_async_copy(cg_ref, coef_ref, sem.at[1])
    a.start()
    b.start()
    a.wait()
    b.wait()


def per_device(S, M, latent, verifying_truth, mix_weight, coefficients, land_mask):
    _, V, N = latent.shape
    T = N // L
    E = N + 2 * L
    nc = len(chunk_plan(T))
    dma = pltpu.SemaphoreType.DMA
    vm = pltpu.VMEM
    anyspec = pl.BlockSpec(memory_space=pltpu.HBM)
    vspec = pl.BlockSpec(memory_space=pltpu.VMEM)
    def hold(x):
        return pltpu.with_memory_space_constraint(x, pltpu.HBM)

    grad, cg = pl.pallas_call(
        functools.partial(kernel, S, M, T),
        out_shape=(jax.ShapeDtypeStruct((V, N), f32), jax.ShapeDtypeStruct((5, 2, N), f32)),
        in_specs=[anyspec] * 5,
        out_specs=(vspec, vspec),
        scratch_shapes=[
            vm((V, E), bf16), vm((V, E), f32), vm((V, E), f32),
            vm((V, E), bf16), vm((V, E), f32), vm((V, E), f32),
            vm((M, V, N), bf16), vm((V, N), bf16), vm((2, 5, 2, L), f32),
            vm((V, E), f32), vm((V, E), f32), vm((V, E), bf16),
            vm((V, E), f32), vm((V, E), bf16),
            vm((2, 2, V, L), bf16), vm((2, 2, V, L), bf16), vm((2, M, 5, N), bf16),
            vm((V, 2, V), bf16), vm((5, 2, N), f32), vm((N,), jnp.int32),
            dma((8,)), dma((4,)), dma((4,)), dma((2,)), dma((2,)),
            dma((M // 2, nc)), dma((nc,)), dma((M // 2, nc)), dma((M, nc)),
            dma((M,)), dma((M,)), dma((3, M)), dma((3, M)),
        ],
        compiler_params=pltpu.CompilerParams(collective_id=0, has_side_effects=True,
                                             vmem_limit_bytes=40 * 1024 * 1024),
    )(hold(latent), hold(verifying_truth), hold(jnp.transpose(mix_weight, (1, 0, 2))),
      hold(jnp.transpose(coefficients, (1, 0, 2))), hold(land_mask))
    grad, cg = pl.pallas_call(
        write_out,
        out_shape=(jax.ShapeDtypeStruct((V, 1, N), f32), jax.ShapeDtypeStruct((5, 2, N), f32)),
        in_specs=[pl.BlockSpec(memory_space=pl.ANY)] * 2,
        out_specs=(anyspec, anyspec),
        scratch_shapes=[dma((2,))],
        compiler_params=pltpu.CompilerParams(vmem_limit_bytes=1024 * 1024),
    )(grad, cg)
    return jnp.transpose(grad, (1, 0, 2)), jnp.transpose(cg, (1, 0, 2))


def solution(mesh):
    in_specs = (
        P("members", None, "space"),
        P(None, "space"),
        P(),
        P(None, None, "space"),
        P("space"),
    )
    out_specs = (P("members", None, "space"), P(None, None, "space"))
    return jax.shard_map(
        functools.partial(per_device, mesh.shape["space"], mesh.shape["members"]),
        mesh=mesh, in_specs=in_specs, out_specs=out_specs, check_vma=False
    )
```
